32 devices in a mesh: leaf: 2 (over core), prow: 2 (over x), pcol: 8 (over z, y).
Axes of the slice: x: 2, y: 2, z: 4, core: 2. Of those that a mesh axis runs over, the one named last changes fastest.
Arguments:
- known_above: bfloat16 [2, 2, 256, 256], P('prow'), may hold values from -6 to 6
- seed_top: float32 [2, 2, 8, 2, 256, 256], P('leaf', 'prow', 'pcol'), may hold values from -6 to 6
- seed_mid: float32 [2, 2, 8, 2, 256, 256], P('leaf', 'prow', 'pcol'), may hold values from -6 to 6
- seed_low: float32 [2, 2, 8, 2, 256, 256], P('leaf', 'prow', 'pcol'), may hold values from -6 to 6
- inverse_top: bfloat16 [2, 2, 8, 2, 256, 256], P('leaf', 'prow', 'pcol'), may hold values from -0.375 to 0.375
- middle_inverses: bfloat16 [2, 2, 8, 2, 256, 256], P('leaf', 'prow', 'pcol'), may hold values from -0.375 to 0.375
- inverse_low: bfloat16 [2, 2, 8, 2, 256, 256], P('leaf', 'prow', 'pcol'), may hold values from -0.375 to 0.375
- tiles_top: bfloat16 [2, 2, 8, 58, 256, 256], P('leaf', 'prow', 'pcol'), may hold values from -0.046875 to 0.046875
- tiles_mid: bfloat16 [2, 2, 8, 58, 256, 256], P('leaf', 'prow', 'pcol'), may hold values from -0.046875 to 0.046875
- tiles_low: bfloat16 [2, 2, 8, 58, 256, 256], P('leaf', 'prow', 'pcol'), may hold values from -0.046875 to 0.046875
- top_source_rows: int32 [2, 2, 8, 58], P('leaf', 'prow', 'pcol'), may hold values from 0 to 1
- source_mid: int32 [2, 2, 8, 58], P('leaf', 'prow', 'pcol'), may hold values from 0 to 33
- lowest_source_rows: int32 [2, 2, 8, 58], P('leaf', 'prow', 'pcol'), may hold values from 0 to 49
- target_top: int32 [2, 2, 8, 58], P('leaf', 'prow', 'pcol'), may hold values from 0 to 3
- target_mid: int32 [2, 2, 8, 58], P('leaf', 'prow', 'pcol'), may hold values from 0 to 3
- target_low: int32 [2, 2, 8, 58], P('leaf', 'prow', 'pcol'), may hold values from 0 to 3
Outputs:
- solved_top: float32 [2, 2, 8, 2, 256, 256], P('leaf', 'prow', 'pcol')
- solved_mid: float32 [2, 2, 8, 2, 256, 256], P('leaf', 'prow', 'pcol')
- solved_low: float32 [2, 2, 8, 2, 256, 256], P('leaf', 'prow', 'pcol')
The draws below stay inside these ranges and needn't reach their ends.
All inputs are finite; a program needn't handle non-finite values.
Results may differ from the reference program's by a relative error of at most 0.015.
Values may be sent and summed in bfloat16 or wider, within the bound.
A program may use at most 192 MiB of HBM per device.

```python
import jax
import jax.numpy as jnp
from jax import lax

NS = 256
R = 256
TILES = 58
CBD = 2
UPD = 2
CB = 4
ROWS_MID = 34
ROWS_LOW = 50
N_LEAF = 2
N_PROW = 2
N_PCOL = 8


def place_ends(result, own_key, smallest, high):
    longest = result.shape.index(max(result.shape))
    spots = []
    for shift in (0, 1):
        where = [jax.random.randint(jax.random.fold_in(own_key, axis), (), 0, length) for axis, length in enumerate(result.shape)]
        where[longest] = (where[longest] + shift) % result.shape[longest]
        spots.append(tuple(where))
    return result.at[spots[0]].set(smallest).at[spots[1]].set(high)


def shard_levels(own_key, extent, pieces, low, largest):
    gain = 1.0
    for position, blocks in pieces:
        heights = jax.random.uniform(jax.random.fold_in(jax.random.fold_in(own_key, 6), position), (blocks,), jnp.float32, low / len(pieces), largest / len(pieces))
        gain = gain * jnp.repeat(jnp.exp(heights), extent[position] // blocks).reshape((-1,) + (1,) * (len(extent) - 1 - position))
    return gain


def centred(key, dims, deviation, most, split=(), kind=jnp.bfloat16):
    drawn = deviation * jax.random.normal(key, dims, jnp.float32)
    if split:
        drawn = drawn * shard_levels(key, dims, split, -0.22, 0.18)
    return jnp.clip(drawn, -most, most).astype(kind)


def setup_inputs(seed: int = 0) -> dict:
    arg_keys = jax.random.split(jax.random.key(seed), 17)
    return {
        "known_above": centred(arg_keys[0], (N_PROW, UPD, R, NS), 1.0, 6.0, ((0, 2),)),
        "seed_top": centred(arg_keys[1], (N_LEAF, N_PROW, N_PCOL, CBD, R, NS), 1.0, 6.0, ((0, 2), (1, 2), (2, 8)), jnp.float32),
        "seed_mid": centred(arg_keys[2], (N_LEAF, N_PROW, N_PCOL, CBD, R, NS), 1.0, 6.0, ((0, 2), (1, 2), (2, 8)), jnp.float32),
        "seed_low": centred(arg_keys[3], (N_LEAF, N_PROW, N_PCOL, CBD, R, NS), 1.0, 6.0, ((0, 2), (1, 2), (2, 8)), jnp.float32),
        "inverse_top": centred(arg_keys[4], (N_LEAF, N_PROW, N_PCOL, CBD, NS, NS), NS ** -0.5, 0.375, ((0, 2), (1, 2), (2, 8))),
        "middle_inverses": centred(arg_keys[5], (N_LEAF, N_PROW, N_PCOL, CBD, NS, NS), NS ** -0.5, 0.375, ((0, 2), (1, 2), (2, 8))),
        "inverse_low": centred(arg_keys[6], (N_LEAF, N_PROW, N_PCOL, CBD, NS, NS), NS ** -0.5, 0.375, ((0, 2), (1, 2), (2, 8))),
        "tiles_top": centred(arg_keys[7], (N_LEAF, N_PROW, N_PCOL, TILES, NS, NS), (2 * TILES * NS // CBD) ** -0.5, 0.046875, ((0, 2), (1, 2), (2, 8))),
        "tiles_mid": centred(arg_keys[8], (N_LEAF, N_PROW, N_PCOL, TILES, NS, NS), (2 * TILES * NS // CBD) ** -0.5, 0.046875, ((0, 2), (1, 2), (2, 8))),
        "tiles_low": centred(arg_keys[9], (N_LEAF, N_PROW, N_PCOL, TILES, NS, NS), (2 * TILES * NS // CBD) ** -0.5, 0.046875, ((0, 2), (1, 2), (2, 8))),
        "top_source_rows": place_ends(jax.random.randint(arg_keys[10], (N_LEAF, N_PROW, N_PCOL, TILES), 0, UPD), jax.random.fold_in(arg_keys[10], 1), 0, UPD - 1).astype(jnp.int32),
        "source_mid": place_ends(jax.random.randint(arg_keys[11], (N_LEAF, N_PROW, N_PCOL, TILES), 0, ROWS_MID), jax.random.fold_in(arg_keys[11], 1), 0, ROWS_MID - 1).astype(jnp.int32),
        "lowest_source_rows": place_ends(jax.random.randint(arg_keys[12], (N_LEAF, N_PROW, N_PCOL, TILES), 0, ROWS_LOW), jax.random.fold_in(arg_keys[12], 1), 0, ROWS_LOW - 1).astype(jnp.int32),
        "target_top": place_ends(jax.random.randint(arg_keys[13], (N_LEAF, N_PROW, N_PCOL, TILES), 0, CB), jax.random.fold_in(arg_keys[13], 1), 0, CB - 1).astype(jnp.int32),
        "target_mid": place_ends(jax.random.randint(arg_keys[14], (N_LEAF, N_PROW, N_PCOL, TILES), 0, CB), jax.random.fold_in(arg_keys[14], 1), 0, CB - 1).astype(jnp.int32),
        "target_low": place_ends(jax.random.randint(arg_keys[15], (N_LEAF, N_PROW, N_PCOL, TILES), 0, CB), jax.random.fold_in(arg_keys[15], 1), 0, CB - 1).astype(jnp.int32),
    }


def level_solve(row_list, tiles, source, target, right_side, inverse):
    n_leaf, n_prow, n_pcol, count_tiles = source.shape
    per_dev = right_side.shape[3]
    columns = n_prow * per_dev
    width = right_side.shape[4]
    depth = right_side.shape[5]
    leaf_ids = jnp.arange(n_leaf, dtype=jnp.int32)[:, None, None]

    def one_prow(acc, items):
        tile_block, src, tgt, rows_here = items
        picked = rows_here[leaf_ids, src]
        products = jnp.einsum("lctra,lctab->lctrb", picked.astype(jnp.float32), tile_block.astype(jnp.float32), precision=lax.Precision.HIGHEST)
        choice_mask = (tgt[:, :, None, :] == jnp.arange(columns, dtype=jnp.int32)[None, None, :, None]).astype(jnp.float32)
        part = jnp.einsum("lcmt,lctrb->lcmrb", choice_mask, products, precision=lax.Precision.HIGHEST)
        part = lax.optimization_barrier(part.astype(jnp.bfloat16)).astype(jnp.float32)
        return acc + part, None

    start = jnp.zeros((n_leaf, n_pcol, columns, width, depth), jnp.float32)
    items = (jnp.transpose(tiles, (1, 0, 2, 3, 4, 5)), jnp.transpose(source, (1, 0, 2, 3)), jnp.transpose(target, (1, 0, 2, 3)), row_list)
    total, unused = lax.scan(one_prow, start, items)
    sums = jnp.transpose(total.reshape(n_leaf, n_pcol, n_prow, per_dev, width, depth), (0, 2, 1, 3, 4, 5))
    reduced = (right_side - sums).astype(jnp.bfloat16)
    return jnp.einsum("lpcdrb,lpcdab->lpcdra", reduced.astype(jnp.float32), inverse.astype(jnp.float32), precision=lax.Precision.HIGHEST)


def extend_shared(row_list, solved_state):
    n_leaf, n_prow, n_pcol, per_dev, width, depth = solved_state.shape
    rounded = solved_state.astype(jnp.bfloat16)
    fresh = jnp.transpose(rounded, (1, 0, 2, 3, 4, 5)).reshape(n_prow, 1, n_leaf * n_pcol * per_dev, width, depth)
    fresh = jnp.broadcast_to(fresh, (n_prow, n_leaf, n_leaf * n_pcol * per_dev, width, depth))
    return jnp.concatenate([row_list, fresh], axis=2)


def extend_own(row_list, solved_state):
    n_leaf, n_prow, n_pcol, per_dev, width, depth = solved_state.shape
    rounded = solved_state.astype(jnp.bfloat16)
    fresh = jnp.transpose(rounded, (1, 0, 2, 3, 4, 5)).reshape(n_prow, n_leaf, n_pcol * per_dev, width, depth)
    return jnp.concatenate([row_list, fresh], axis=2)


def reference(known_above, seed_top, seed_mid, seed_low, inverse_top, middle_inverses, inverse_low, tiles_top, tiles_mid, tiles_low, top_source_rows, source_mid, lowest_source_rows, target_top, target_mid, target_low):
    n_leaf = seed_top.shape[0]
    n_prow, upper, width, depth = known_above.shape
    row_list = jnp.broadcast_to(known_above[:, None], (n_prow, n_leaf, upper, width, depth))
    solved_top = level_solve(row_list, tiles_top, top_source_rows, target_top, seed_top, inverse_top)
    row_list = extend_shared(row_list, solved_top)
    solved_mid = level_solve(row_list, tiles_mid, source_mid, target_mid, seed_mid, middle_inverses)
    row_list = extend_own(row_list, solved_mid)
    solved_low = level_solve(row_list, tiles_low, lowest_source_rows, target_low, seed_low, inverse_low)
    return (solved_top, solved_mid, solved_low)
```

```python
import functools

import jax
import jax.numpy as jnp
from jax import lax
from jax.experimental import pallas as pl
from jax.experimental.pallas import tpu as pltpu
from jax.sharding import PartitionSpec as P

MESH = pl.DeviceIdType.MESH
CHUNKS = 4
HOP = 3.2
SPACING = 3.0
GROUP = 29
PAIR = 2


def kernel(dims, *refs):
    n_leaf, n_prow, n_pcol, n_tiles, per_dev, upper, width, depth = dims
    rows = width // CHUNKS
    columns = n_prow * per_dev
    line = n_pcol // PAIR
    (known, *rest) = refs
    seeds, rest = rest[:3], rest[3:]
    inverses, rest = rest[:3], rest[3:]
    tiles_hbm, rest = rest[:3], rest[3:]
    sources, rest = rest[:3], rest[3:]
    targets, rest = rest[:3], rest[3:]
    outs, rest = rest[:3], rest[3:]
    tiles, rest = rest[:3], rest[3:]
    top_store, rest = rest[:CHUNKS], rest[CHUNKS:]
    mid_store, rest = rest[:CHUNKS], rest[CHUNKS:]
    seg, x_send, x_recv, seed_vm, inv_vm, out_vm = rest[:6]
    tile_sem, in_sem, out_sem, xs_sem, xr_sem, g_send, g_recv = rest[6:]

    leaf = lax.axis_index("leaf")
    prow = lax.axis_index("prow")
    pcol = lax.axis_index("pcol")
    z = pcol // PAIR
    y = pcol % PAIR

    cuts = [0, *range(GROUP, n_tiles, GROUP), n_tiles]
    parts = list(zip(cuts[:-1], cuts[1:]))

    def tile_copy(level, part):
        lo, hi = parts[part] if level == 0 else (0, n_tiles)
        return pltpu.make_async_copy(
            tiles_hbm[level].at[pl.ds(lo, hi - lo)],
            tiles[level].at[pl.ds(lo, hi - lo)],
            tile_sem.at[level, part],
        )

    def seed_copy(level):
        return pltpu.make_async_copy(seeds[level], seed_vm.at[level], in_sem.at[0, level])

    def inverse_copy(level):
        return pltpu.make_async_copy(inverses[level], inv_vm.at[level], in_sem.at[1, level])

    def out_copy(level, chunk):
        here = pl.ds(chunk * rows, rows)
        return pltpu.make_async_copy(
            out_vm.at[level, :, here, :], outs[level].at[:, here, :], out_sem.at[level, chunk]
        )

    for part in range(len(parts)):
        tile_copy(0, part).start()
    for level in range(3):
        if level > 0:
            tile_copy(level, 0).start()
        seed_copy(level).start()
        inverse_copy(level).start()

    barrier = pltpu.get_barrier_semaphore()

    def greet(where):
        pl.semaphore_signal(barrier, inc=1, device_id=where, device_id_type=MESH)

    for off in range(1, n_prow):
        greet({"prow": lax.rem(prow + off, n_prow)})
    for off in range(1, n_leaf):
        greet({"leaf": lax.rem(leaf + off, n_leaf)})
    greet({"pcol": z * PAIR + (1 - y)})

    @pl.when(z > 0)
    def _():
        greet({"pcol": pcol - PAIR})

    @pl.when(z < line - 1)
    def _():
        greet({"pcol": pcol + PAIR})

    for chunk in range(CHUNKS):
        top_store[chunk][0:upper] = known[:, chunk * rows : (chunk + 1) * rows, :]
    seg[n_tiles] = jnp.zeros((rows, depth), jnp.float32)

    near = (z > 0).astype(jnp.int32) + (z < line - 1).astype(jnp.int32)
    pl.semaphore_wait(barrier, (n_prow - 1) + (n_leaf - 1) + 1 + near)

    def row_block(level, chunk, source):
        if level == 0:
            return known[source, chunk * rows : (chunk + 1) * rows, :]
        if level == 1:
            return top_store[chunk][source]
        count = upper + n_leaf * n_pcol * per_dev
        first = top_store[chunk][jnp.minimum(source, count - 1)]
        second = mid_store[chunk][jnp.maximum(source - count, 0)]
        return lax.select(source < count, first, second)

    def products(level, chunk):
        def step(t, last):
            source = sources[level][t]
            target = targets[level][t]
            product = jnp.dot(
                row_block(level, chunk, source), tiles[level][t], preferred_element_type=jnp.float32
            )
            before = last[0]
            for m in range(1, columns):
                before = jnp.where(target == m, last[m], before)
            seg[t] = seg[before] + product
            return tuple(jnp.where(target == m, t, last[m]) for m in range(columns))

        def group(i, last):
            for j in range(GROUP):
                last = step(i * GROUP + j, last)
            return last

        last = tuple(jnp.int32(n_tiles) for _ in range(columns))
        if chunk == 0 and level > 0:
            tile_copy(level, 0).wait()
        spans = parts if level == 0 and chunk == 0 else [(0, n_tiles)]
        for part, (lo, hi) in enumerate(spans):
            if level == 0 and chunk == 0:
                tile_copy(0, part).wait()
            last = lax.fori_loop(lo // GROUP, hi // GROUP, group, last)
            for t in range(hi // GROUP * GROUP, hi):
                last = step(jnp.int32(t), last)

        def partial(q, d):
            where = last[d]
            for other in range(1, n_prow):
                where = jnp.where(q == other, last[other * per_dev + d], where)
            return seg[where].astype(jnp.bfloat16)

        for off in range(1, n_prow):
            q = lax.rem(prow + off, n_prow)
            for d in range(per_dev):
                x_send[level, chunk, off, d] = partial(q, d)
            x_copy(level, chunk, off).start()
        for d in range(per_dev):
            x_send[level, chunk, 0, d] = partial(prow, d)

    def x_copy(level, chunk, off):
        return pltpu.make_async_remote_copy(
            src_ref=x_send.at[level, chunk, off],
            dst_ref=x_recv.at[level, chunk, off - 1],
            send_sem=xs_sem.at[level, chunk, off - 1],
            recv_sem=xr_sem.at[level, chunk, off - 1],
            device_id={"prow": lax.rem(prow + off, n_prow)},
            device_id_type=MESH,
        )

    def piece(g, chunk, l, c):
        if g == 0:
            return top_store[chunk].at[pl.ds(upper + (l * n_pcol + c) * per_dev, per_dev)]
        return mid_store[chunk].at[pl.ds(c * per_dev, per_dev)]

    def solve(level, chunk):
        for off in range(1, n_prow):
            x_copy(level, chunk, off).wait_recv()
        here = slice(chunk * rows, (chunk + 1) * rows)
        if chunk == 0:
            seed_copy(level).wait()
            inverse_copy(level).wait()
        for d in range(per_dev):
            sums = x_send[level, chunk, 0, d].astype(jnp.float32)
            for off in range(1, n_prow):
                sums = sums + x_recv[level, chunk, off - 1, d].astype(jnp.float32)
            reduced = (seed_vm[level, d, here, :] - sums).astype(jnp.bfloat16)
            solved = lax.dot_general(
                reduced,
                inv_vm[level, d],
                (((1,), (1,)), ((), ())),
                preferred_element_type=jnp.float32,
            )
            out_vm[level, d, here, :] = solved
            if level == 0:
                top_store[chunk][upper + (leaf * n_pcol + pcol) * per_dev + d] = solved.astype(
                    jnp.bfloat16
                )
            elif level == 1:
                mid_store[chunk][pcol * per_dev + d] = solved.astype(jnp.bfloat16)

        out_copy(level, chunk).start()

    UP, DOWN, ACROSS, SIBLING = 0, 1, 2, 3

    def copy(g, chunk, way, c, l=None):
        where = {
            UP: {"pcol": pcol + PAIR},
            DOWN: {"pcol": pcol - PAIR},
            ACROSS: {"pcol": z * PAIR + (1 - y)},
            SIBLING: {"leaf": 1 - leaf},
        }[way]
        l = leaf if l is None else l
        return pltpu.make_async_remote_copy(
            src_ref=piece(g, chunk, l, c),
            dst_ref=piece(g, chunk, l, c),
            send_sem=g_send.at[g, chunk, way, c],
            recv_sem=g_recv.at[g, chunk, l, c],
            device_id=where,
            device_id_type=MESH,
        )

    def arrived(g, chunk, c, l=None):
        copy(g, chunk, SIBLING, c, l).wait_recv()

    def hand_on(g, chunk, o, same, act):
        c = o * PAIR + (y if same else 1 - y)
        may_turn = chunk % 2 == 1
        turned = (o == 0) | (o == line - 1)

        def when(condition, way):
            @pl.when(condition)
            def _():
                act(copy(g, chunk, way, c))

        up = (z < line - 1) & (o <= z)
        down = (z > 0) & (o >= z)
        if same:
            when(up, UP)
            when(down, DOWN)
            if may_turn:
                when((o == z) | jnp.logical_not(turned), ACROSS)
            else:
                act(copy(g, chunk, ACROSS, c))
        elif may_turn:
            when(turned & up, UP)
            when(turned & down, DOWN)
        if g == 0:
            act(copy(g, chunk, SIBLING, c))

    def start(dma):
        dma.start()

    def wait_send(dma):
        dma.wait_send()

    def launch(g, chunk):
        hand_on(g, chunk, z, True, start)

    def take(g, chunk, o, same):
        arrived(g, chunk, o * PAIR + (y if same else 1 - y))
        hand_on(g, chunk, o, same, start)

    def take_at(g, chunk, s, same):
        @pl.when(z >= s)
        def _():
            take(g, chunk, z - s, same)

        @pl.when(z + s < line)
        def _():
            take(g, chunk, z + s, same)

    def step_gather(g, chunk, s):
        if s < line:
            take_at(g, chunk, s, True)
        if s == 1:
            take(g, chunk, z, False)
        else:
            take_at(g, chunk, s - 1, False)

    def finish(g, chunk):
        if g == 0:
            for c in range(n_pcol):
                arrived(g, chunk, c, 1 - leaf)

    events = []

    def at(time, act, *which):
        events.append((time, len(events), act, which))

    free = 0.0
    solved_at = [5.0 + 1.5 * chunk for chunk in range(CHUNKS)]
    for chunk in range(CHUNKS):
        at(0.0, products, 0, chunk)
    for g in range(2):
        for chunk in range(CHUNKS):
            begin = max(solved_at[chunk] + 0.1, free)
            free = begin + SPACING
            at(solved_at[chunk], solve, g, chunk)
            at(begin, launch, g, chunk)
            for s in range(1, line + 1):
                at(begin + s * HOP, step_gather, g, chunk, s)
            done = begin + (line + 0.4) * HOP
            at(done, finish, g, chunk)
            at(done, products, g + 1, chunk)
            solved_at[chunk] = done + 4.0
    for chunk in range(CHUNKS):
        at(solved_at[chunk], solve, 2, chunk)
    for _, _, act, which in sorted(events, key=lambda e: e[:2]):
        act(*which)

    for level in range(3):
        for chunk in range(CHUNKS):
            out_copy(level, chunk).wait()
            for off in range(1, n_prow):
                x_copy(level, chunk, off).wait_send()
    for g in range(2):
        for chunk in range(CHUNKS):

            def left(o, carry):
                hand_on(g, chunk, o, True, wait_send)
                hand_on(g, chunk, o, False, wait_send)
                return carry

            lax.fori_loop(0, line, left, 0)


def settle(*refs):
    sources, outs, held, sem = refs[:3], refs[3:6], refs[6], refs[7]

    def taken(i):
        return pltpu.make_async_copy(sources[i], held.at[i], sem.at[0, i])

    def given(i):
        return pltpu.make_async_copy(held.at[i], outs[i], sem.at[1, i])

    for i in range(3):
        taken(i).start()
    for i in range(3):
        taken(i).wait()
        given(i).start()
    for i in range(3):
        given(i).wait()


def local(*args):
    n_leaf, n_prow, n_pcol = (lax.axis_size(a) for a in ("leaf", "prow", "pcol"))
    known = args[0][0]
    seeds = [a[0, 0, 0] for a in args[1:4]]
    inverses = [a[0, 0, 0] for a in args[4:7]]
    tiles = [a[0, 0, 0] for a in args[7:10]]
    sources = [a[0, 0, 0] for a in args[10:13]]
    targets = [a[0, 0, 0] for a in args[13:16]]
    upper, width, depth = known.shape
    n_tiles = tiles[0].shape[0]
    per_dev = seeds[0].shape[0]
    rows = width // CHUNKS
    vmem = pl.BlockSpec(memory_space=pltpu.VMEM)
    smem = pl.BlockSpec(memory_space=pltpu.SMEM)
    hbm = pl.BlockSpec(memory_space=pl.ANY)
    bf16, f32 = jnp.bfloat16, jnp.float32
    dims = (n_leaf, n_prow, n_pcol, n_tiles, per_dev, upper, width, depth)
    outs = pl.pallas_call(
        functools.partial(kernel, dims),
        out_shape=[jax.ShapeDtypeStruct((per_dev, width, depth), f32)] * 3,
        in_specs=[vmem] + [hbm] * 9 + [smem] * 6,
        out_specs=[hbm] * 3,
        scratch_shapes=[pltpu.VMEM((n_tiles, depth, depth), bf16)] * 3
        + [pltpu.VMEM((upper + n_leaf * n_pcol * per_dev, rows, depth), bf16)] * CHUNKS
        + [pltpu.VMEM((n_pcol * per_dev, rows, depth), bf16)] * CHUNKS
        + [
            pltpu.VMEM((n_tiles + 1, rows, depth), f32),
            pltpu.VMEM((3, CHUNKS, n_prow, per_dev, rows, depth), bf16),
            pltpu.VMEM((3, CHUNKS, n_prow - 1, per_dev, rows, depth), bf16),
            pltpu.VMEM((3, per_dev, width, depth), f32),
            pltpu.VMEM((3, per_dev, depth, depth), bf16),
            pltpu.VMEM((3, per_dev, width, depth), f32),
            pltpu.SemaphoreType.DMA((3, pl.cdiv(n_tiles, GROUP))),
            pltpu.SemaphoreType.DMA((2, 3)),
            pltpu.SemaphoreType.DMA((3, CHUNKS)),
            pltpu.SemaphoreType.DMA((3, CHUNKS, n_prow - 1)),
            pltpu.SemaphoreType.DMA((3, CHUNKS, n_prow - 1)),
            pltpu.SemaphoreType.DMA((2, CHUNKS, 4, n_pcol)),
            pltpu.SemaphoreType.DMA((2, CHUNKS, n_leaf, n_pcol)),
        ],
        compiler_params=pltpu.CompilerParams(
            collective_id=0, has_side_effects=True, vmem_limit_bytes=67043328
        ),
        name="window",
    )(known, *seeds, *inverses, *tiles, *sources, *targets)
    outs = pl.pallas_call(
        settle,
        out_shape=[jax.ShapeDtypeStruct((per_dev, width, depth), f32)] * 3,
        in_specs=[hbm] * 3,
        out_specs=[hbm] * 3,
        scratch_shapes=[
            pltpu.VMEM((3, per_dev, width, depth), f32),
            pltpu.SemaphoreType.DMA((2, 3)),
        ],
        name="settle",
    )(*outs)
    return tuple(o[None, None, None] for o in outs)


def solution(mesh):
    blocks = P("leaf", "prow", "pcol", None, None, None)
    lists = P("leaf", "prow", "pcol", None)
    in_specs = (P("prow", None, None, None),) + (blocks,) * 9 + (lists,) * 6
    return jax.shard_map(
        local, mesh=mesh, in_specs=in_specs, out_specs=(blocks,) * 3, check_vma=False
    )
```
